128 devices in a mesh: ctx: 8 (over y, x_hi), head: 16 (over x_lo, z, core).
Axes of the slice: x: 4 (x_hi: 2, x_lo: 2; x = x_hi * 2 + x_lo), y: 4, z: 4, core: 2. Of those that a mesh axis runs over, the one named last changes fastest.
Arguments:
- queries: bfloat16 [2, 4096, 4096], P(None, 'ctx', 'head'), may hold values from -6 to 6
- keys: bfloat16 [2, 4096, 4096], P(None, 'ctx', 'head'), may hold values from -6 to 6
- values: bfloat16 [2, 4096, 4096], P(None, 'ctx', 'head'), may hold values from -6 to 6
- rates: float32 [16, 2, 4096], P('head', None, 'ctx'), may hold values from 0.05 to 1
- w_gate: float32 [16, 256, 512], P('head'), may hold values from -0.375 to 0.375
- w_up: float32 [16, 256, 512], P('head'), may hold values from -0.375 to 0.375
- w_down: float32 [16, 512, 256], P('head'), may hold values from -0.25 to 0.25
- gains: float32 [16, 256], P('head'), may hold values from 0.25 to 0.6
- out_proj: bfloat16 [4096, 4096], P('head'), may hold values from -0.125 to 0.125
Outputs:
- output: bfloat16 [2, 4096, 4096], P(None, 'ctx', 'head')
The draws below stay inside these ranges and needn't reach their ends.
All inputs are finite; a program needn't handle non-finite values.
Results may differ from the reference program's by a relative error of at most 0.0051.
Values may be sent and summed in bfloat16 or wider, within the bound.
A program may use at most 128 MiB of HBM per device.

```python
import math
import jax
import jax.numpy as jnp
from jax import lax

HD = 256
FH = 512
WINDOW = 256
NS_ITERS = 5
GROUPS = 2
HEADS = 16
D = 4096
GROUP_TOK = 4096


def raised(entries, stream_key, source, target, parts, factor):
    def block_of(position):
        return (jnp.arange(entries.shape[position]) // (entries.shape[position] // parts)).reshape((-1,) + (1,) * (entries.ndim - 1 - position))

    near = jax.random.permutation(stream_key, parts)[block_of(target)]
    second = (block_of(target) + parts // 2) % parts
    return jnp.where((block_of(source) == near) | (block_of(source) == second), factor * entries, entries)


def level_of(key, shape, cuts, low, high):
    def one(position, blocks):
        steps = jax.random.uniform(jax.random.fold_in(jax.random.fold_in(key, 6), position), (blocks,), jnp.float32, low / len(cuts), high / len(cuts))
        return jnp.repeat(jnp.exp(steps), shape[position] // blocks).reshape((-1,) + (1,) * (len(shape) - position - 1))

    level = one(*cuts[0])
    for cut in cuts[1:]:
        level = level * one(*cut)
    return level


def normal_values(rng, extent, spread, bound, cuts=(), kind=jnp.bfloat16):
    values = spread * jax.random.normal(rng, extent, jnp.float32)
    if cuts:
        values = values * level_of(rng, extent, cuts, -0.22, 0.18)
    return jnp.clip(values, -bound, bound).astype(kind)


def bell_draw_with(own_key, dims, scale, limit, cuts, heavy, kind=jnp.bfloat16):
    drawn = scale * jax.random.normal(own_key, dims, jnp.float32)
    if cuts:
        drawn = drawn * level_of(own_key, dims, cuts, -0.22, 0.18)
    return jnp.clip(raised(drawn, jax.random.fold_in(own_key, 3), *heavy), -limit, limit).astype(kind)


def setup_inputs(seed: int = 0) -> dict:
    key_of = jax.random.split(jax.random.key(seed), 10)
    return {
        "queries": normal_values(key_of[0], (GROUPS, GROUP_TOK, D), 1.0, 6.0, ((1, 8), (2, 16))),
        "keys": normal_values(key_of[1], (GROUPS, GROUP_TOK, D), 1.0, 6.0, ((1, 8), (2, 16))),
        "values": normal_values(key_of[2], (GROUPS, GROUP_TOK, D), 1.0, 6.0, ((1, 8), (2, 16))),
        "rates": jnp.clip(jnp.exp(math.log(1.0) - 2.9957323 * jax.random.uniform(key_of[3], (HEADS, GROUPS, GROUP_TOK), jnp.float32) ** level_of(key_of[3], (HEADS, GROUPS, GROUP_TOK), ((0, 16), (2, 8)), -0.2, 0.2)), 0.05, 1.0),
        "w_gate": normal_values(key_of[4], (HEADS, HD, FH), HD ** -0.5, 0.375, ((0, 16),), jnp.float32),
        "w_up": normal_values(key_of[5], (HEADS, HD, FH), HD ** -0.5, 0.375, ((0, 16),), jnp.float32),
        "w_down": normal_values(key_of[6], (HEADS, FH, HD), FH ** -0.5, 0.25, ((0, 16),), jnp.float32),
        "gains": jnp.clip(0.25 + 0.35000002 * jax.random.uniform(key_of[7], (HEADS, HD), jnp.float32) ** level_of(key_of[7], (HEADS, HD), ((0, 16),), -0.2, 0.2), 0.25, 0.6),
        "out_proj": bell_draw_with(key_of[8], (D, D), D ** -0.5, 0.125, ((0, 16),), (0, 1, 16, 2.0)),
    }


highest = lax.Precision.HIGHEST
attn_temp = 5.0
step_size = 0.5
quintic_one = 3.4445
quintic_two = -4.775
quintic_three = 2.0315

def unit_rows(matrix):
    return matrix / jnp.sqrt(lax.optimization_barrier(jnp.sum(matrix * matrix, axis=-1, keepdims=True)) + 1e-06)

def exact_dot(left, right):
    return jnp.dot(left, right, precision=highest, preferred_element_type=jnp.float32)

def fast_grads(key_unit, value_rows, rate_rows, w_gate, w_up, w_down):
    gate_pre = exact_dot(key_unit, w_gate)
    up_pre = exact_dot(key_unit, w_up)
    sigma = jax.nn.sigmoid(gate_pre)
    gate_act = gate_pre * sigma
    hidden = gate_act * up_pre
    target = rate_rows[:, None] * value_rows
    grad_down = exact_dot(hidden.T, target)
    back_hidden = exact_dot(target, w_down.T)
    slope = sigma * (1.0 + gate_pre * (1.0 - sigma))
    grad_gate = exact_dot(key_unit.T, back_hidden * up_pre * slope)
    grad_up = exact_dot(key_unit.T, back_hidden * gate_act)
    return jnp.stack([grad_gate, grad_up, grad_down.T])

def orthogonal(grads):
    norms = jnp.sqrt(lax.optimization_barrier(jnp.sum(grads * grads, axis=(1, 2), keepdims=True))) + 1e-06
    iterate = grads / norms
    for sweep_at in range(NS_ITERS):
        gram = jnp.einsum('mik,mjk->mij', iterate, iterate, precision=highest)
        poly = quintic_two * gram + quintic_three * jnp.einsum('mij,mjk->mik', gram, gram, precision=highest)
        iterate = quintic_one * iterate + jnp.einsum('mij,mjk->mik', poly, iterate, precision=highest)
    return iterate

def apply_fast(query_unit, w_gate, w_up, w_down):
    gate_pre = exact_dot(query_unit, w_gate)
    gate_act = gate_pre * jax.nn.sigmoid(gate_pre)
    return exact_dot(gate_act * exact_dot(query_unit, w_up), w_down)

def window_attention(query_half, key_half, value_rows):
    total_rows = query_half.shape[0]
    key_pad = jnp.concatenate([jnp.zeros((WINDOW, HD), key_half.dtype), key_half], axis=0)
    value_pad = jnp.concatenate([jnp.zeros((WINDOW, HD), value_rows.dtype), value_rows], axis=0)

    def one_block(start):
        query_block = lax.dynamic_slice_in_dim(query_half, start, WINDOW, 0)
        key_block = lax.dynamic_slice_in_dim(key_pad, start, 2 * WINDOW, 0)
        value_block = lax.dynamic_slice_in_dim(value_pad, start, 2 * WINDOW, 0)
        scores = lax.dot_general(query_block, key_block, (((1,), (1,)), ((), ())), preferred_element_type=jnp.float32)
        query_pos = jnp.arange(WINDOW, dtype=jnp.int32)[:, None]
        key_pos = jnp.arange(2 * WINDOW, dtype=jnp.int32)[None, :]
        distance = query_pos + WINDOW - key_pos
        valid = (distance >= 0) & (distance < WINDOW) & (key_pos + start >= WINDOW)
        weights = jnp.where(valid, jnp.exp(attn_temp * (scores - 1.0)), 0.0)
        probs = (weights / lax.optimization_barrier(jnp.sum(weights, axis=-1, keepdims=True))).astype(jnp.bfloat16)
        return jnp.dot(probs, value_block, preferred_element_type=jnp.float32)
    starts = (jnp.arange(total_rows // WINDOW) * WINDOW).astype(jnp.int32)
    return lax.map(one_block, starts).reshape(total_rows, HD)

def head_path(operands):
    query_rows, key_rows, value_rows, rate_rows, gate_now, up_now, down_now, gain_row = operands
    query_unit = unit_rows(query_rows.astype(jnp.float32))
    key_unit = unit_rows(key_rows.astype(jnp.float32))
    attended = window_attention(query_unit.astype(jnp.bfloat16), key_unit.astype(jnp.bfloat16), value_rows)
    pieces = []
    for group_at in range(GROUPS):
        lower = group_at * GROUP_TOK
        upper = lower + GROUP_TOK
        grads = fast_grads(key_unit[lower:upper], value_rows[lower:upper].astype(jnp.float32), rate_rows[group_at], gate_now, up_now, down_now)
        ortho = orthogonal(grads)
        gate_now = gate_now + step_size * ortho[0]
        up_now = up_now + step_size * ortho[1]
        down_now = down_now + step_size * ortho[2].T
        pieces.append(apply_fast(query_unit[lower:upper], gate_now, up_now, down_now))
    fast_out = jnp.concatenate(pieces, axis=0)
    normed = fast_out * lax.rsqrt(lax.optimization_barrier(jnp.mean(fast_out * fast_out, axis=-1, keepdims=True)) + 1e-05) * gain_row
    return (attended + normed).astype(jnp.bfloat16)

def reference(queries, keys, values, rates, w_gate, w_up, w_down, gains, out_proj):
    total_rows = GROUPS * GROUP_TOK

    def to_heads(array):
        return array.reshape(total_rows, HEADS, HD).transpose(1, 0, 2)
    combined = lax.map(head_path, (to_heads(queries), to_heads(keys), to_heads(values), rates, w_gate, w_up, w_down, gains))
    flat = combined.transpose(1, 0, 2).reshape(total_rows, HEADS * HD)
    result = jnp.dot(flat, out_proj, preferred_element_type=jnp.float32).astype(jnp.bfloat16)
    return result.reshape(GROUPS, GROUP_TOK, D)
```

```python
import functools
import jax
import jax.numpy as jnp
from jax import lax
from jax.experimental import pallas as pl
from jax.experimental.pallas import tpu as pltpu
from jax.sharding import PartitionSpec as P

WINDOW = 256
NS_ITERS = 5
MESH = pl.DeviceIdType.MESH
bf16 = jnp.bfloat16
f32 = jnp.float32

NN = (((1,), (0,)), ((), ()))
NT = (((1,), (1,)), ((), ()))
COPIES = 120


def split(x):
    high = x.astype(bf16)
    return high, (x - high.astype(f32)).astype(bf16)


def dot1(a, b, dims=NN):
    return lax.dot_general(a, b, dims, preferred_element_type=f32)


def dot3(a, b, dims=NN):
    return dot1(a[0], b[0], dims) + (dot1(a[0], b[1], dims) + dot1(a[1], b[0], dims))


def unit_rows(x):
    return x / jnp.sqrt(jnp.sum(x * x, axis=-1, keepdims=True) + 1e-06)


def kernel(
    q_ref, k_ref, v_ref, rate_ref, gate_ref, up_ref, downt_ref, gain_ref, proj_ref,
    out_ref,
    gate_now, up_now, down_now, sums, part, yslot, xown, xslot, full, halo, attended, projg, gath, iterate,
    send_sem, recv_sem, local_sem,
):
    ctx = lax.axis_index("ctx")
    head = lax.axis_index("head")
    yi, xh = ctx // 2, ctx % 2
    xl, z, core = head // 8, (head // 2) % 4, head % 2
    first = ctx == 0

    barrier = pltpu.get_barrier_semaphore()
    for d in range(1, 8):
        pl.semaphore_signal(barrier, inc=1, device_id={"ctx": lax.rem(ctx + d, 8)}, device_id_type=MESH)
    for d in range(1, 16):
        pl.semaphore_signal(barrier, inc=1, device_id={"head": lax.rem(head + d, 16)}, device_id_type=MESH)

    started = []

    def send(src, dst, where):
        at = len(started)
        copy = pltpu.make_async_remote_copy(
            src_ref=src, dst_ref=dst, send_sem=send_sem.at[at], recv_sem=recv_sem.at[at],
            device_id=where, device_id_type=MESH,
        )
        copy.start()
        started.append(copy)
        return copy

    def rows64(index):
        return pl.ds(pl.multiple_of(index * 64, 64), 64)

    def halo_send(group):
        there = {"ctx": lax.rem(ctx + 1, 8)}
        return [
            send(ref.at[group, pl.ds(256, 256)], halo.at[group, at], there)
            for at, ref in enumerate((k_ref, v_ref))
        ]

    gate_now[...] = gate_ref[0]
    up_now[...] = up_ref[0]
    down_now[...] = downt_ref[0]

    def reduce_start(group, which, value):
        part[group, which] = value.astype(bf16)
        own = []
        for d in (2, 1, 3):
            there = lax.rem(yi + d, 4)
            own.append(
                send(
                    part.at[group, which, rows64(there)],
                    yslot.at[group, which, d - 1],
                    {"ctx": there * 2 + xh},
                )
            )
        return own

    def fast_grads(group, ready=None):
        key_unit = unit_rows(k_ref[group].astype(f32))
        key_two = split(key_unit)
        key_t = split(key_unit.T)
        gate_pre = dot3(key_two, split(gate_now[...]))
        up_pre = dot3(key_two, split(up_now[...]))
        target = rate_ref[group] * v_ref[group].astype(f32)
        sigma = jax.nn.sigmoid(gate_pre)
        gate_act = gate_pre * sigma
        grad_down = dot3(split(target.T), split(gate_act * up_pre))
        if ready is not None:
            ready()
        sends = {2: reduce_start(group, 2, grad_down)}
        back = dot3(split(target), split(down_now[...]))
        sends[1] = reduce_start(group, 1, dot3(key_t, split(back * gate_act)))
        slope = sigma * (1.0 + gate_pre * (1.0 - sigma))
        sends[0] = reduce_start(group, 0, dot3(key_t, split(back * up_pre * slope)))
        return sends

    def reduce_second(group, which, sends):
        for copy in sends:
            copy.wait_recv()
        total = part[group, which, rows64(yi)].astype(f32)
        for slot in range(3):
            total = total + yslot[group, which, slot].astype(f32)
        xown[group, which] = total.astype(bf16)
        return send(xown.at[group, which], xslot.at[group, which], {"ctx": yi * 2 + (1 - xh)})

    def reduce_third(group, which, copy):
        copy.wait_recv()
        total = xown[group, which].astype(f32) + xslot[group, which].astype(f32)
        full[group, which, rows64(yi)] = total.astype(bf16)
        return [
            send(
                full.at[group, which, rows64(yi)],
                full.at[group, which, rows64(yi)],
                {"ctx": lax.rem(yi + d, 4) * 2 + xh},
            )
            for d in (2, 1, 3)
        ]

    def orthogonal(group, which, now):
        grads = full[group, which].astype(f32)
        norm = jnp.sqrt(jnp.sum(grads * grads, keepdims=True)) + 1e-06
        iterate[...] = grads / norm

        def sweep(_, carry):
            x = iterate[...]
            x2 = split(x)
            gram = dot3(x2, x2, NT)
            g2 = split(gram)
            poly = -4.775 * gram + 2.0315 * dot3(g2, g2)
            iterate[...] = 3.4445 * x + dot3(split(poly), x2)
            return carry

        lax.fori_loop(0, NS_ITERS, sweep, 0)
        now[...] = now[...] + 0.5 * iterate[...]

    def attend(group):
        if group == 0:
            prior = 0
        else:
            prior = jnp.where(first, 0, 1)
        query = unit_rows(q_ref[group].astype(f32)).astype(bf16)
        key = unit_rows(k_ref[group].astype(f32)).astype(bf16)
        halo_key = unit_rows(halo[prior, 0].astype(f32)).astype(bf16)
        query_pos = lax.broadcasted_iota(jnp.int32, (256, 512), 0)
        key_pos = lax.broadcasted_iota(jnp.int32, (256, 512), 1)
        distance = query_pos + WINDOW - key_pos
        band = (distance >= 0) & (distance < WINDOW)
        for block in range(2):
            if block == 0:
                keys = jnp.concatenate([halo_key, key[:256]], axis=0)
                vals = jnp.concatenate([halo[prior, 1], v_ref[group, 0:256]], axis=0)
            else:
                keys = key
                vals = v_ref[group]
            scores = dot1(query[block * 256 : block * 256 + 256], keys, NT)
            valid = band
            if block == 0 and group == 0:
                valid = band & (key_pos >= jnp.where(first, WINDOW, 0))
            weights = jnp.where(valid, jnp.exp(5.0 * (scores - 1.0)), 0.0)
            probs = (weights / jnp.sum(weights, axis=-1, keepdims=True)).astype(bf16)
            attended[group, block * 256 : block * 256 + 256] = dot1(probs, vals)

    def apply_fast(group):
        query = split(unit_rows(q_ref[group].astype(f32)))
        gate_pre = dot3(query, split(gate_now[...]))
        hidden = gate_pre * jax.nn.sigmoid(gate_pre) * dot3(query, split(up_now[...]))
        fast = dot3(split(hidden), split(down_now[...]), NT)
        normed = fast * lax.rsqrt(jnp.mean(fast * fast, axis=-1, keepdims=True) + 1e-05) * gain_ref[...]
        gath[group, head] = (attended[group] + normed).astype(bf16)

    def name(xl_at, z_at, core_at):
        return xl_at * 8 + lax.rem(z_at + 4, 4) * 2 + core_at

    sibling = {"head": name(xl, z, 1 - core)}
    above = {"head": name(xl, z + 1, core)}
    below = {"head": name(xl, z - 1, core)}
    across = {"head": name(1 - xl, z, core)}

    def block_send(group, owner, where, rows=None):
        ref = gath.at[group, owner] if rows is None else gath.at[group, owner, rows]
        return send(ref, ref, where)

    def gather_one(group):
        return {
            "sib": block_send(group, head, sibling),
            "x": block_send(group, head, across),
            "zp": block_send(group, head, above),
            "zm": block_send(group, head, below),
        }

    def gather_two(group, c):
        c["zp"].wait_recv()
        c["f1"] = block_send(group, name(xl, z - 1, core), above, pl.ds(0, 256))
        c["s1"] = block_send(group, name(xl, z - 1, core), sibling)
        c["zm"].wait_recv()
        c["f2"] = block_send(group, name(xl, z + 1, core), below, pl.ds(256, 256))
        c["s2"] = block_send(group, name(xl, z + 1, core), sibling)
        c["x"].wait_recv()
        c["xp"] = block_send(group, name(1 - xl, z, core), above)
        c["xm"] = block_send(group, name(1 - xl, z, core), below)
        c["s3"] = block_send(group, name(1 - xl, z, core), sibling)

    def gather_three(group, c):
        c["f1"].wait_recv()
        c["f2"].wait_recv()
        c["x2"] = block_send(group, name(xl, z + 2, core), across)
        c["s4"] = block_send(group, name(xl, z + 2, core), sibling)
        c["xp"].wait_recv()
        c["s5"] = block_send(group, name(1 - xl, z - 1, core), sibling)
        c["xm"].wait_recv()
        c["s6"] = block_send(group, name(1 - xl, z + 1, core), sibling)

    def gather_four(group, c):
        c["x2"].wait_recv()
        c["s7"] = block_send(group, name(1 - xl, z + 2, core), sibling)

    def arrived(c):
        for key in ("sib", "s1", "s2", "s3", "s4", "s5", "s6", "s7"):
            c[key].wait_recv()

    def project(group):
        total = None
        for at in range(16):
            term = dot1(gath[group, at], projg[at])
            total = term if total is None else total + term
        out_ref[group] = total.astype(bf16)

    halos = []

    def on_ready():
        pl.semaphore_wait(barrier, 22)

    def on_ready_one():
        return

    sends = fast_grads(0, on_ready)
    halos.append(halo_send(0))
    cross = {which: reduce_second(0, which, sends[which]) for which in (2, 1, 0)}
    spread = {which: reduce_third(0, which, cross[which]) for which in (2, 1, 0)}
    halos.append(halo_send(1))
    mine = pltpu.make_async_copy(
        proj_ref.at[:, pl.ds(pl.multiple_of(head * 256, 256), 256)], projg.at[head], local_sem
    )
    mine.start()
    exchange = []
    for d in range(1, 16):
        there = lax.rem(head + d, 16)
        exchange.append(
            send(
                proj_ref.at[:, pl.ds(pl.multiple_of(there * 256, 256), 256)],
                projg.at[head],
                {"head": there},
            )
        )
    for copy in halos[0]:
        copy.wait_recv()
    attend(0)
    for which, now in ((2, down_now), (1, up_now), (0, gate_now)):
        for copy in spread[which]:
            copy.wait_recv()
        orthogonal(0, which, now)

    sends = fast_grads(1)
    apply_fast(0)
    near = gather_one(0)
    cross = {which: reduce_second(1, which, sends[which]) for which in (2, 1, 0)}
    for copy in halos[1]:
        copy.wait_recv()
    spread = {which: reduce_third(1, which, cross[which]) for which in (2, 1, 0)}
    attend(1)
    gather_two(0, near)
    for which, now in ((2, down_now), (1, up_now), (0, gate_now)):
        for copy in spread[which]:
            copy.wait_recv()
        orthogonal(1, which, now)
        if which == 2:
            gather_three(0, near)
        if which == 1:
            gather_four(0, near)
    apply_fast(1)
    last = gather_one(1)
    mine.wait()
    for copy in exchange:
        copy.wait_recv()
    arrived(near)
    project(0)
    gather_two(1, last)
    gather_three(1, last)
    gather_four(1, last)
    arrived(last)
    project(1)
    for copy in started:
        copy.wait_send()


def body(queries, keys, values, rates, w_gate, w_up, w_down, gains, out_proj):
    groups, rows, width = queries.shape
    hidden = w_gate.shape[2]
    vmem = pl.BlockSpec(memory_space=pltpu.VMEM)
    return pl.pallas_call(
        kernel,
        out_shape=jax.ShapeDtypeStruct((groups, rows, width), bf16),
        in_specs=[vmem] * 8 + [pl.BlockSpec(memory_space=pl.ANY)],
        out_specs=vmem,
        scratch_shapes=[
            pltpu.VMEM((width, hidden), f32),
            pltpu.VMEM((width, hidden), f32),
            pltpu.VMEM((width, hidden), f32),
            pltpu.VMEM((8, 128), f32),
            pltpu.VMEM((2, 3, width, hidden), bf16),
            pltpu.VMEM((2, 3, 3, 64, hidden), bf16),
            pltpu.VMEM((2, 3, 64, hidden), bf16),
            pltpu.VMEM((2, 3, 64, hidden), bf16),
            pltpu.VMEM((2, 3, width, hidden), bf16),
            pltpu.VMEM((2, 2, WINDOW, width), bf16),
            pltpu.VMEM((2, rows, width), f32),
            pltpu.VMEM((16, width, width), bf16),
            pltpu.VMEM((2, 16, rows, width), bf16),
            pltpu.VMEM((width, hidden), f32),
            pltpu.SemaphoreType.DMA((COPIES,)),
            pltpu.SemaphoreType.DMA((COPIES,)),
            pltpu.SemaphoreType.DMA,
        ],
        compiler_params=pltpu.CompilerParams(
            collective_id=0, has_side_effects=True, vmem_limit_bytes=62 * 1024 * 1024
        ),
    )(
        queries, keys, values, rates[0][:, :, None], w_gate, w_up, jnp.swapaxes(w_down, 1, 2), gains, out_proj
    )


def solution(mesh):
    return jax.shard_map(
        body,
        mesh=mesh,
        in_specs=(
            P(None, "ctx", "head"),
            P(None, "ctx", "head"),
            P(None, "ctx", "head"),
            P("head", None, "ctx"),
            P("head", None, None),
            P("head", None, None),
            P("head", None, None),
            P("head", None),
            P("head", None),
        ),
        out_specs=P(None, "ctx", "head"),
        check_vma=False,
    )
```

```python
import functools
import jax
import jax.numpy as jnp
from jax import lax
from jax.experimental import pallas as pl
from jax.experimental.pallas import tpu as pltpu
from jax.sharding import PartitionSpec as P

WINDOW = 256
NS_ITERS = 5
MESH = pl.DeviceIdType.MESH
bf16 = jnp.bfloat16
f32 = jnp.float32

NN = (((1,), (0,)), ((), ()))
NT = (((1,), (1,)), ((), ()))
COPIES = 128


def split(x):
    high = x.astype(bf16)
    return high, (x - high.astype(f32)).astype(bf16)


def dot1(a, b, dims=NN):
    return lax.dot_general(a, b, dims, preferred_element_type=f32)


def dot3(a, b, dims=NN):
    axis = dims[0][1][0]
    left = jnp.concatenate([a[0], a[0], a[1]], axis=1)
    right = jnp.concatenate([b[0], b[1], b[0]], axis=axis)
    return dot1(left, right, dims)


def unit_rows(x):
    return x / jnp.sqrt(jnp.sum(x * x, axis=-1, keepdims=True) + 1e-06)


def kernel(
    q_ref, k_ref, v_ref, rate_ref, gate_ref, up_ref, down_ref, gain_ref, proj_ref,
    out_ref,
    gate_now, up_now, down_now, sums, part, yslot, xown, xslot, full, halo, attended, projg, gath, iterate,
    send_sem, recv_sem, local_sem,
):
    ctx = lax.axis_index("ctx")
    head = lax.axis_index("head")
    yi, xh = ctx // 2, ctx % 2
    xl, z, core = head // 8, (head // 2) % 4, head % 2
    first = ctx == 0

    barrier = pltpu.get_barrier_semaphore()
    for d in range(1, 8):
        pl.semaphore_signal(barrier, inc=1, device_id={"ctx": lax.rem(ctx + d, 8)}, device_id_type=MESH)
    for d in range(1, 16):
        pl.semaphore_signal(barrier, inc=1, device_id={"head": lax.rem(head + d, 16)}, device_id_type=MESH)

    started = []

    def send(src, dst, where):
        at = len(started)
        copy = pltpu.make_async_remote_copy(
            src_ref=src, dst_ref=dst, send_sem=send_sem.at[at], recv_sem=recv_sem.at[at],
            device_id=where, device_id_type=MESH,
        )
        copy.start()
        started.append(copy)
        return copy

    y_up = {"ctx": lax.rem(yi + 1, 4) * 2 + xh}
    y_down = {"ctx": lax.rem(yi + 3, 4) * 2 + xh}

    def rows64(index):
        return pl.ds(pl.multiple_of(index * 64, 64), 64)

    def halo_send(group):
        there = {"ctx": lax.rem(ctx + 1, 8)}
        return [
            send(ref.at[group, pl.ds(256, 256)], halo.at[group, at], there)
            for at, ref in enumerate((k_ref, v_ref))
        ]

    gate_now[...] = gate_ref[0]
    up_now[...] = up_ref[0]
    down_now[...] = down_ref[0].T

    def reduce_start(group, which, value):
        part[group, which] = value.astype(bf16)
        own = []
        for d in (2, 1, 3):
            there = lax.rem(yi + d, 4)
            own.append(
                send(
                    part.at[group, which, rows64(there)],
                    yslot.at[group, which, d - 1],
                    {"ctx": there * 2 + xh},
                )
            )
        return own

    def fast_grads(group, ready=None):
        key_unit = unit_rows(k_ref[group].astype(f32))
        key_two = split(key_unit)
        key_t = split(key_unit.T)
        gate_pre = dot3(key_two, split(gate_now[...]))
        up_pre = dot3(key_two, split(up_now[...]))
        if ready is not None:
            ready()
        rate_rows = jnp.broadcast_to(rate_ref[0, group : group + 1, :], (128, 512)).T[:, :1]
        target = rate_rows * v_ref[group].astype(f32)
        sigma = jax.nn.sigmoid(gate_pre)
        gate_act = gate_pre * sigma
        grad_down = dot3(split(target.T), split(gate_act * up_pre))
        sends = {2: reduce_start(group, 2, grad_down)}
        back = dot3(split(target), split(down_now[...]))
        sends[1] = reduce_start(group, 1, dot3(key_t, split(back * gate_act)))
        slope = sigma * (1.0 + gate_pre * (1.0 - sigma))
        sends[0] = reduce_start(group, 0, dot3(key_t, split(back * up_pre * slope)))
        return sends

    def reduce_second(group, which, sends):
        for copy in sends:
            copy.wait_recv()
        total = part[group, which, rows64(yi)].astype(f32)
        for slot in range(3):
            total = total + yslot[group, which, slot].astype(f32)
        xown[group, which] = total.astype(bf16)
        return send(xown.at[group, which], xslot.at[group, which], {"ctx": yi * 2 + (1 - xh)})

    def reduce_third(group, which, copy):
        copy.wait_recv()
        total = xown[group, which].astype(f32) + xslot[group, which].astype(f32)
        full[group, which, rows64(yi)] = total.astype(bf16)
        ref = full.at[group, which, rows64(yi)]
        return [send(ref, ref, y_up), send(ref, ref, y_down)]

    def reduce_fourth(group, which, copies):
        relays = []
        for copy, source, half, where in ((copies[0], yi + 3, 0, y_up), (copies[1], yi + 1, 32, y_down)):
            copy.wait_recv()
            start = pl.multiple_of(lax.rem(source, 4) * 64 + half, 32)
            ref = full.at[group, which, pl.ds(start, 32)]
            relays.append(send(ref, ref, where))
        return relays

    def ortho_start(group, places):
        for at in places:
            grads = full[group, at].astype(f32)
            norm = jnp.sqrt(jnp.sum(grads * grads, keepdims=True)) + 1e-06
            iterate[at] = grads / norm

    def ortho_sweeps(places, count):
        def sweep(_, carry):
            x2 = {at: split(iterate[at]) for at in places}
            gram = {at: dot3(x2[at], x2[at], NT) for at in places}
            g2 = {at: split(gram[at]) for at in places}
            poly = {at: -4.775 * gram[at] + 2.0315 * dot3(g2[at], g2[at]) for at in places}
            p2 = {at: split(poly[at]) for at in places}
            for at in places:
                iterate[at] = 3.4445 * iterate[at] + dot3(p2[at], x2[at])
            return carry

        lax.fori_loop(0, count, sweep, 0)

    def ortho_finish(places):
        for at in places:
            now = (gate_now, up_now, down_now)[at]
            now[...] = now[...] + 0.5 * iterate[at]

    def update(group, spread):
        relays = {2: reduce_fourth(group, 2, spread[2])}
        for copy in relays[2]:
            copy.wait_recv()
        relays[1] = reduce_fourth(group, 1, spread[1])
        relays[0] = reduce_fourth(group, 0, spread[0])
        for which in (1, 0):
            for copy in relays[which]:
                copy.wait_recv()
        yield
        ortho_start(group, (2, 1, 0))
        ortho_sweeps((2, 1, 0), NS_ITERS)
        ortho_finish((2, 1, 0))
        yield

    def attend(group):
        if group == 0:
            prior = 0
        else:
            prior = jnp.where(first, 0, 1)
        query = unit_rows(q_ref[group].astype(f32)).astype(bf16)
        key = unit_rows(k_ref[group].astype(f32)).astype(bf16)
        halo_key = unit_rows(halo[prior, 0].astype(f32)).astype(bf16)
        query_pos = lax.broadcasted_iota(jnp.int32, (256, 512), 0)
        key_pos = lax.broadcasted_iota(jnp.int32, (256, 512), 1)
        distance = query_pos + WINDOW - key_pos
        band = (distance >= 0) & (distance < WINDOW)
        for block in range(2):
            if block == 0:
                keys = jnp.concatenate([halo_key, key[:256]], axis=0)
                vals = jnp.concatenate([halo[prior, 1], v_ref[group, 0:256]], axis=0)
            else:
                keys = key
                vals = v_ref[group]
            scores = dot1(query[block * 256 : block * 256 + 256], keys, NT)
            valid = band
            if block == 0 and group == 0:
                valid = band & (key_pos >= jnp.where(first, WINDOW, 0))
            weights = jnp.where(valid, jnp.exp(5.0 * (scores - 1.0)), 0.0)
            probs = (weights / jnp.sum(weights, axis=-1, keepdims=True)).astype(bf16)
            attended[group, block * 256 : block * 256 + 256] = dot1(probs, vals)

    def apply_fast(group, half):
        rows = pl.ds(half * 256, 256)
        query = split(unit_rows(q_ref[group, rows].astype(f32)))
        gate_pre = dot3(query, split(gate_now[...]))
        hidden = gate_pre * jax.nn.sigmoid(gate_pre) * dot3(query, split(up_now[...]))
        fast = dot3(split(hidden), split(down_now[...]), NT)
        normed = fast * lax.rsqrt(jnp.mean(fast * fast, axis=-1, keepdims=True) + 1e-05) * gain_ref[...]
        gath[group, head, rows] = (attended[group, rows] + normed).astype(bf16)

    def name(xl_at, z_at, core_at):
        return xl_at * 8 + lax.rem(z_at + 4, 4) * 2 + core_at

    sibling = {"head": name(xl, z, 1 - core)}
    above = {"head": name(xl, z + 1, core)}
    below = {"head": name(xl, z - 1, core)}
    across = {"head": name(1 - xl, z, core)}

    def block_send(group, owner, where, rows=None):
        ref = gath.at[group, owner] if rows is None else gath.at[group, owner, rows]
        return send(ref, ref, where)

    def half_rows(half):
        return pl.ds(half * 256, 256)

    def gather_z(group, half, c):
        c["zp", half] = block_send(group, head, above, half_rows(half))
        c["zm", half] = block_send(group, head, below, half_rows(half))

    def gather_x(group, half, c):
        c["x", half] = block_send(group, head, across, half_rows(half))

    def gather_sibling(group, c):
        c["sib"] = block_send(group, head, sibling)

    def relay_x(group, half, c):
        c["x", half].wait_recv()
        c["xp", half] = block_send(group, name(1 - xl, z, core), above, half_rows(half))
        c["xm", half] = block_send(group, name(1 - xl, z, core), below, half_rows(half))

    def relay_z(group, half, c):
        if half == 0:
            c["zp", 0].wait_recv()
            c["f", 0] = block_send(group, name(xl, z - 1, core), above, half_rows(0))
        else:
            c["zm", 1].wait_recv()
            c["f", 1] = block_send(group, name(xl, z + 1, core), below, half_rows(1))

    def relay_far(group, half, c):
        c["f", half].wait_recv()
        c["x2", half] = block_send(group, name(xl, z + 2, core), across, half_rows(half))

    def share_near(group, c):
        c["zp", 1].wait_recv()
        c["s1"] = block_send(group, name(xl, z - 1, core), sibling)
        c["zm", 0].wait_recv()
        c["s2"] = block_send(group, name(xl, z + 1, core), sibling)

    def share_across(group, c):
        c["s3"] = block_send(group, name(1 - xl, z, core), sibling)

    def share_far(group, c):
        c["s4"] = block_send(group, name(xl, z + 2, core), sibling)

    def share_sides(group, c):
        for half in range(2):
            c["xp", half].wait_recv()
        c["s5"] = block_send(group, name(1 - xl, z - 1, core), sibling)
        for half in range(2):
            c["xm", half].wait_recv()
        c["s6"] = block_send(group, name(1 - xl, z + 1, core), sibling)

    def share_last(group, c):
        for half in range(2):
            c["x2", half].wait_recv()
        c["s7"] = block_send(group, name(1 - xl, z + 2, core), sibling)

    own_order = (
        (xl, z), (xl, z - 1), (xl, z + 1), (1 - xl, z), (xl, z + 2), (1 - xl, z - 1), (1 - xl, z + 1), (1 - xl, z + 2)
    )
    shared = ("sib", "s1", "s2", "s3", "s4", "s5", "s6", "s7")

    def project(group, total, own, c):
        for at in own:
            owner = name(*own_order[at], core)
            term = dot1(gath[group, owner], projg[owner])
            total = term if total is None else total + term
        for at in own:
            c[shared[at]].wait_recv()
            owner = name(*own_order[at], 1 - core)
            total = total + dot1(gath[group, owner], projg[owner])
        return total

    mine = pltpu.make_async_copy(
        proj_ref.at[:, pl.ds(pl.multiple_of(head * 256, 256), 256)], projg.at[head], local_sem
    )
    exchange = []

    def exchange_with(there):
        exchange.append(
            send(
                proj_ref.at[:, pl.ds(pl.multiple_of(there * 256, 256), 256)],
                projg.at[head],
                {"head": there},
            )
        )

    def exchange_across(which):
        for d in which:
            exchange_with((1 - xl) * 8 + lax.rem(head + d, 8))

    def on_ready():
        pl.semaphore_wait(barrier, 22)
        mine.start()
        for d in range(1, 8):
            exchange_with(xl * 8 + lax.rem(head + d, 8))
        exchange_across(range(3))

    order = (2, 1, 0)
    sends = fast_grads(0, on_ready)
    cross = {which: reduce_second(0, which, sends[which]) for which in order}
    spread = {which: reduce_third(0, which, cross[which]) for which in order}
    steps = update(0, spread)
    next(steps)
    halos = [halo_send(0), halo_send(1)]
    next(steps)
    exchange_across(range(3, 8))

    sends = fast_grads(1)
    near, last = {}, {}
    for copy in halos[0]:
        copy.wait_recv()
    attend(0)
    for half in range(2):
        apply_fast(0, half)
        gather_z(0, half, near)
    gather_sibling(0, near)
    cross = {which: reduce_second(1, which, sends[which]) for which in order}
    for half in range(2):
        gather_x(0, half, near)
    spread = {which: reduce_third(1, which, cross[which]) for which in order}
    for half in range(2):
        relay_z(0, half, near)
    steps = update(1, spread)
    next(steps)
    share_near(0, near)
    for half in range(2):
        relay_x(0, half, near)
        relay_far(0, half, near)
    share_across(0, near)
    share_far(0, near)
    for copy in halos[1]:
        copy.wait_recv()
    attend(1)
    next(steps)
    share_sides(0, near)
    share_last(0, near)
    for half in range(2):
        apply_fast(1, half)
        gather_x(1, half, last)
        gather_z(1, half, last)
    gather_sibling(1, last)
    mine.wait()
    for copy in exchange:
        copy.wait_recv()
    out_ref[0] = project(0, None, range(8), near).astype(bf16)
    for half in range(2):
        relay_x(1, half, last)
        relay_z(1, half, last)
    share_near(1, last)
    share_across(1, last)
    total = project(1, None, range(4), last)
    for half in range(2):
        relay_far(1, half, last)
    share_far(1, last)
    share_sides(1, last)
    total = project(1, total, range(4, 7), last)
    share_last(1, last)
    out_ref[1] = project(1, total, range(7, 8), last).astype(bf16)
    for copy in started:
        copy.wait_send()


def body(queries, keys, values, rates, w_gate, w_up, w_down, gains, out_proj):
    groups, rows, width = queries.shape
    hidden = w_gate.shape[2]
    vmem = pl.BlockSpec(memory_space=pltpu.VMEM)
    return pl.pallas_call(
        kernel,
        out_shape=jax.ShapeDtypeStruct((groups, rows, width), bf16),
        in_specs=[vmem] * 8 + [pl.BlockSpec(memory_space=pl.ANY)],
        out_specs=vmem,
        scratch_shapes=[
            pltpu.VMEM((width, hidden), f32),
            pltpu.VMEM((width, hidden), f32),
            pltpu.VMEM((width, hidden), f32),
            pltpu.VMEM((8, 128), f32),
            pltpu.VMEM((2, 3, width, hidden), bf16),
            pltpu.VMEM((2, 3, 3, 64, hidden), bf16),
            pltpu.VMEM((2, 3, 64, hidden), bf16),
            pltpu.VMEM((2, 3, 64, hidden), bf16),
            pltpu.VMEM((2, 3, width, hidden), bf16),
            pltpu.VMEM((2, 2, WINDOW, width), bf16),
            pltpu.VMEM((2, rows, width), f32),
            pltpu.VMEM((16, width, width), bf16),
            pltpu.VMEM((2, 16, rows, width), bf16),
            pltpu.VMEM((3, width, hidden), f32),
            pltpu.SemaphoreType.DMA((COPIES,)),
            pltpu.SemaphoreType.DMA((COPIES,)),
            pltpu.SemaphoreType.DMA,
        ],
        compiler_params=pltpu.CompilerParams(
            collective_id=0, has_side_effects=True, vmem_limit_bytes=62 * 1024 * 1024
        ),
    )(
        queries, keys, values, rates, w_gate, w_up, w_down, gains, out_proj
    )


def solution(mesh):
    return jax.shard_map(
        body,
        mesh=mesh,
        in_specs=(
            P(None, "ctx", "head"),
            P(None, "ctx", "head"),
            P(None, "ctx", "head"),
            P("head", None, "ctx"),
            P("head", None, None),
            P("head", None, None),
            P("head", None, None),
            P("head", None),
            P("head", None),
        ),
        out_specs=P(None, "ctx", "head"),
        check_vma=False,
    )
```

```python
import functools
import jax
import jax.numpy as jnp
from jax import lax
from jax.experimental import pallas as pl
from jax.experimental.pallas import tpu as pltpu
from jax.sharding import PartitionSpec as P

WINDOW = 256
NS_ITERS = 5
MESH = pl.DeviceIdType.MESH
bf16 = jnp.bfloat16
f32 = jnp.float32

NN = (((1,), (0,)), ((), ()))
NT = (((1,), (1,)), ((), ()))
COPIES = 128


def split(x):
    high = x.astype(bf16)
    return high, (x - high.astype(f32)).astype(bf16)


def dot1(a, b, dims=NN):
    return lax.dot_general(a, b, dims, preferred_element_type=f32)


def dot3(a, b, dims=NN):
    axis = dims[0][1][0]
    left = jnp.concatenate([a[0], a[0], a[1]], axis=1)
    right = jnp.concatenate([b[0], b[1], b[0]], axis=axis)
    return dot1(left, right, dims)


def mirrored(whole, side):
    return whole + (side + side.T)


def unit_rows(x):
    return x / jnp.sqrt(jnp.sum(x * x, axis=-1, keepdims=True) + 1e-06)


def kernel(
    q_ref, k_ref, v_ref, rate_ref, gate_ref, up_ref, down_ref, gain_ref, proj_ref,
    out_ref,
    gate_now, up_now, down_now, part, yslot, xown, xslot, full, halo, attended, projg, gath, iterate,
    send_sem, recv_sem, local_sem,
):
    ctx = lax.axis_index("ctx")
    head = lax.axis_index("head")
    yi, xh = ctx // 2, ctx % 2
    xl, z, core = head // 8, (head // 2) % 4, head % 2
    first = ctx == 0

    barrier = pltpu.get_barrier_semaphore()
    for d in range(1, 8):
        pl.semaphore_signal(barrier, inc=1, device_id={"ctx": lax.rem(ctx + d, 8)}, device_id_type=MESH)
    for d in range(1, 16):
        pl.semaphore_signal(barrier, inc=1, device_id={"head": lax.rem(head + d, 16)}, device_id_type=MESH)

    started = []

    def send(src, dst, where):
        at = len(started)
        copy = pltpu.make_async_remote_copy(
            src_ref=src, dst_ref=dst, send_sem=send_sem.at[at], recv_sem=recv_sem.at[at],
            device_id=where, device_id_type=MESH,
        )
        copy.start()
        started.append(copy)
        return copy

    def rows64(index):
        return pl.ds(pl.multiple_of(index * 64, 64), 64)

    def halo_send(group):
        there = {"ctx": lax.rem(ctx + 1, 8)}
        return [
            send(ref.at[group, pl.ds(256, 256)], halo.at[group, at], there)
            for at, ref in enumerate((k_ref, v_ref))
        ]

    gate_now[...] = gate_ref[0]
    up_now[...] = up_ref[0]
    down_now[...] = down_ref[0].T

    def reduce_start(group, which, value):
        part[group, which] = value.astype(bf16)
        own = []
        for d in (2, 1, 3):
            there = lax.rem(yi + d, 4)
            own.append(
                send(
                    part.at[group, which, rows64(there)],
                    yslot.at[group, which, d - 1],
                    {"ctx": there * 2 + xh},
                )
            )
        return own

    def fast_grads(group, ready=None):
        key_unit = unit_rows(k_ref[group].astype(f32))
        key_two = split(key_unit)
        key_t = split(key_unit.T)
        gate_pre = dot3(key_two, split(gate_now[...]))
        up_pre = dot3(key_two, split(up_now[...]))
        if ready is not None:
            ready()
        rate_rows = jnp.broadcast_to(rate_ref[0, group : group + 1, :], (128, 512)).T[:, :1]
        target = rate_rows * v_ref[group].astype(f32)
        sigma = jax.nn.sigmoid(gate_pre)
        gate_act = gate_pre * sigma
        grad_down = dot3(split(target.T), split(gate_act * up_pre))
        sends = {2: reduce_start(group, 2, grad_down)}
        back = dot3(split(target), split(down_now[...]))
        sends[1] = reduce_start(group, 1, dot3(key_t, split(back * gate_act)))
        slope = sigma * (1.0 + gate_pre * (1.0 - sigma))
        sends[0] = reduce_start(group, 0, dot3(key_t, split(back * up_pre * slope)))
        return sends

    def reduce_second(group, which, sends):
        for copy in sends:
            copy.wait_recv()
        total = part[group, which, rows64(yi)].astype(f32)
        for slot in range(3):
            total = total + yslot[group, which, slot].astype(f32)
        xown[group, which] = total.astype(bf16)
        return send(xown.at[group, which], xslot.at[group, which], {"ctx": yi * 2 + (1 - xh)})

    def reduce_third(group, which, copy):
        copy.wait_recv()
        total = xown[group, which].astype(f32) + xslot[group, which].astype(f32)
        full[group, which, rows64(yi)] = total.astype(bf16)
        ref = full.at[group, which, rows64(yi)]
        return [send(ref, ref, {"ctx": lax.rem(yi + d, 4) * 2 + xh}) for d in (2, 1, 3)]

    def ortho_start(group, places):
        for at in places:
            grads = full[group, at].astype(f32)
            norm = jnp.sqrt(jnp.sum(grads * grads, keepdims=True)) + 1e-06
            iterate[at] = grads / norm

    def ortho_sweeps(places, count):
        def sweep(_, carry):
            x2 = {at: split(iterate[at]) for at in places}
            gram = {at: mirrored(dot1(x2[at][0], x2[at][0], NT), dot1(x2[at][0], x2[at][1], NT)) for at in places}
            g2 = {at: split(gram[at]) for at in places}
            poly = {
                at: -4.775 * gram[at] + 2.0315 * mirrored(dot1(g2[at][0], g2[at][0]), dot1(g2[at][0], g2[at][1]))
                for at in places
            }
            p2 = {at: split(poly[at]) for at in places}
            for at in places:
                iterate[at] = 3.4445 * iterate[at] + dot3(p2[at], x2[at])
            return carry

        lax.fori_loop(0, count, sweep, 0)

    def ortho_finish(places):
        for at in places:
            now = (gate_now, up_now, down_now)[at]
            now[...] = now[...] + 0.5 * iterate[at]

    def update(group, spread):
        for which in (2, 1, 0):
            for copy in spread[which]:
                copy.wait_recv()
        yield
        ortho_start(group, (2, 1, 0))
        ortho_sweeps((2, 1, 0), NS_ITERS)
        ortho_finish((2, 1, 0))
        yield

    def attend(group):
        if group == 0:
            prior = 0
        else:
            prior = jnp.where(first, 0, 1)
        query = unit_rows(q_ref[group].astype(f32)).astype(bf16)
        key = unit_rows(k_ref[group].astype(f32)).astype(bf16)
        halo_key = unit_rows(halo[prior, 0].astype(f32)).astype(bf16)
        query_pos = lax.broadcasted_iota(jnp.int32, (256, 512), 0)
        key_pos = lax.broadcasted_iota(jnp.int32, (256, 512), 1)
        distance = query_pos + WINDOW - key_pos
        band = (distance >= 0) & (distance < WINDOW)
        for block in range(2):
            if block == 0:
                keys = jnp.concatenate([halo_key, key[:256]], axis=0)
                vals = jnp.concatenate([halo[prior, 1], v_ref[group, 0:256]], axis=0)
            else:
                keys = key
                vals = v_ref[group]
            scores = dot1(query[block * 256 : block * 256 + 256], keys, NT)
            valid = band
            if block == 0 and group == 0:
                valid = band & (key_pos >= jnp.where(first, WINDOW, 0))
            weights = jnp.where(valid, jnp.exp(5.0 * (scores - 1.0)), 0.0)
            probs = (weights / jnp.sum(weights, axis=-1, keepdims=True)).astype(bf16)
            attended[group, block * 256 : block * 256 + 256] = dot1(probs, vals)

    def apply_fast(group, half):
        rows = pl.ds(half * 256, 256)
        query = split(unit_rows(q_ref[group, rows].astype(f32)))
        gate_pre = dot3(query, split(gate_now[...]))
        hidden = gate_pre * jax.nn.sigmoid(gate_pre) * dot3(query, split(up_now[...]))
        fast = dot3(split(hidden), split(down_now[...]), NT)
        normed = fast * lax.rsqrt(jnp.mean(fast * fast, axis=-1, keepdims=True) + 1e-05) * gain_ref[...]
        gath[group, head, rows] = (attended[group, rows] + normed).astype(bf16)

    def name(xl_at, z_at, core_at):
        return xl_at * 8 + lax.rem(z_at + 4, 4) * 2 + core_at

    sibling = {"head": name(xl, z, 1 - core)}
    above = {"head": name(xl, z + 1, core)}
    below = {"head": name(xl, z - 1, core)}
    across = {"head": name(1 - xl, z, core)}

    def block_send(group, owner, where, rows=None):
        ref = gath.at[group, owner] if rows is None else gath.at[group, owner, rows]
        return send(ref, ref, where)

    def half_rows(half):
        return pl.ds(half * 256, 256)

    def gather_z(group, half, c):
        c["zp", half] = block_send(group, head, above, half_rows(half))
        c["zm", half] = block_send(group, head, below, half_rows(half))

    def gather_x(group, half, c):
        c["x", half] = block_send(group, head, across, half_rows(half))

    def gather_sibling(group, c):
        c["sib"] = block_send(group, head, sibling)

    def relay_x(group, half, c):
        c["x", half].wait_recv()
        c["xp", half] = block_send(group, name(1 - xl, z, core), above, half_rows(half))
        c["xm", half] = block_send(group, name(1 - xl, z, core), below, half_rows(half))

    def relay_z(group, half, c):
        if half == 0:
            c["zp", 0].wait_recv()
            c["f", 0] = block_send(group, name(xl, z - 1, core), above, half_rows(0))
        else:
            c["zm", 1].wait_recv()
            c["f", 1] = block_send(group, name(xl, z + 1, core), below, half_rows(1))

    def relay_far(group, half, c):
        c["f", half].wait_recv()
        c["x2", half] = block_send(group, name(xl, z + 2, core), across, half_rows(half))

    def share_near(group, c):
        c["zp", 1].wait_recv()
        c["s1"] = block_send(group, name(xl, z - 1, core), sibling)
        c["zm", 0].wait_recv()
        c["s2"] = block_send(group, name(xl, z + 1, core), sibling)

    def share_across(group, c):
        c["s3"] = block_send(group, name(1 - xl, z, core), sibling)

    def share_far(group, c):
        c["s4"] = block_send(group, name(xl, z + 2, core), sibling)

    def share_sides(group, c):
        for half in range(2):
            c["xp", half].wait_recv()
        c["s5"] = block_send(group, name(1 - xl, z - 1, core), sibling)
        for half in range(2):
            c["xm", half].wait_recv()
        c["s6"] = block_send(group, name(1 - xl, z + 1, core), sibling)

    def share_last(group, c):
        for half in range(2):
            c["x2", half].wait_recv()
        c["s7"] = block_send(group, name(1 - xl, z + 2, core), sibling)

    own_order = (
        (xl, z), (xl, z - 1), (xl, z + 1), (1 - xl, z), (xl, z + 2), (1 - xl, z - 1), (1 - xl, z + 1), (1 - xl, z + 2)
    )
    shared = ("sib", "s1", "s2", "s3", "s4", "s5", "s6", "s7")

    def project(group, total, own, c):
        for at in own:
            owner = name(*own_order[at], core)
            term = dot1(gath[group, owner], projg[owner])
            total = term if total is None else total + term
        for at in own:
            c[shared[at]].wait_recv()
            owner = name(*own_order[at], 1 - core)
            total = total + dot1(gath[group, owner], projg[owner])
        return total

    mine = pltpu.make_async_copy(
        proj_ref.at[:, pl.ds(pl.multiple_of(head * 256, 256), 256)], projg.at[head], local_sem
    )
    exchange = []

    def exchange_with(there):
        exchange.append(
            send(
                proj_ref.at[:, pl.ds(pl.multiple_of(there * 256, 256), 256)],
                projg.at[head],
                {"head": there},
            )
        )

    def exchange_across(which):
        for d in which:
            exchange_with((1 - xl) * 8 + lax.rem(head + d, 8))

    def on_ready():
        pl.semaphore_wait(barrier, 22)
        mine.start()
        for d in range(1, 8):
            exchange_with(xl * 8 + lax.rem(head + d, 8))
        exchange_across(range(3))

    order = (2, 1, 0)
    sends = fast_grads(0, on_ready)
    cross = {which: reduce_second(0, which, sends[which]) for which in order}
    spread = {which: reduce_third(0, which, cross[which]) for which in order}
    steps = update(0, spread)
    next(steps)
    halos = [halo_send(0), halo_send(1)]
    next(steps)
    exchange_across(range(3, 8))

    sends = fast_grads(1)
    near, last = {}, {}
    for copy in halos[0]:
        copy.wait_recv()
    attend(0)
    for half in range(2):
        apply_fast(0, half)
        gather_z(0, half, near)
    gather_sibling(0, near)
    cross = {which: reduce_second(1, which, sends[which]) for which in order}
    for half in range(2):
        gather_x(0, half, near)
    spread = {which: reduce_third(1, which, cross[which]) for which in order}
    for half in range(2):
        relay_z(0, half, near)
    steps = update(1, spread)
    next(steps)
    share_near(0, near)
    for half in range(2):
        relay_x(0, half, near)
        relay_far(0, half, near)
    share_across(0, near)
    share_far(0, near)
    for copy in halos[1]:
        copy.wait_recv()
    attend(1)
    next(steps)
    share_sides(0, near)
    share_last(0, near)
    for half in range(2):
        apply_fast(1, half)
        gather_x(1, half, last)
        gather_z(1, half, last)
    gather_sibling(1, last)
    mine.wait()
    for copy in exchange:
        copy.wait_recv()
    out_ref[0] = project(0, None, range(8), near).astype(bf16)
    for half in range(2):
        relay_x(1, half, last)
        relay_z(1, half, last)
    share_near(1, last)
    share_across(1, last)
    total = project(1, None, range(4), last)
    for half in range(2):
        relay_far(1, half, last)
    share_far(1, last)
    share_sides(1, last)
    total = project(1, total, range(4, 7), last)
    share_last(1, last)
    out_ref[1] = project(1, total, range(7, 8), last).astype(bf16)
    for copy in started:
        copy.wait_send()


def body(queries, keys, values, rates, w_gate, w_up, w_down, gains, out_proj):
    groups, rows, width = queries.shape
    hidden = w_gate.shape[2]
    vmem = pl.BlockSpec(memory_space=pltpu.VMEM)
    return pl.pallas_call(
        kernel,
        out_shape=jax.ShapeDtypeStruct((groups, rows, width), bf16),
        in_specs=[vmem] * 8 + [pl.BlockSpec(memory_space=pl.ANY)],
        out_specs=vmem,
        scratch_shapes=[
            pltpu.VMEM((width, hidden), f32),
            pltpu.VMEM((width, hidden), f32),
            pltpu.VMEM((width, hidden), f32),
            pltpu.VMEM((2, 3, width, hidden), bf16),
            pltpu.VMEM((2, 3, 3, 64, hidden), bf16),
            pltpu.VMEM((2, 3, 64, hidden), bf16),
            pltpu.VMEM((2, 3, 64, hidden), bf16),
            pltpu.VMEM((2, 3, width, hidden), bf16),
            pltpu.VMEM((2, 2, WINDOW, width), bf16),
            pltpu.VMEM((2, rows, width), f32),
            pltpu.VMEM((16, width, width), bf16),
            pltpu.VMEM((2, 16, rows, width), bf16),
            pltpu.VMEM((3, width, hidden), f32),
            pltpu.SemaphoreType.DMA((COPIES,)),
            pltpu.SemaphoreType.DMA((COPIES,)),
            pltpu.SemaphoreType.DMA,
        ],
        compiler_params=pltpu.CompilerParams(
            collective_id=0, has_side_effects=True, vmem_limit_bytes=62 * 1024 * 1024
        ),
    )(
        queries, keys, values, rates, w_gate, w_up, w_down, gains, out_proj
    )


def solution(mesh):
    return jax.shard_map(
        body,
        mesh=mesh,
        in_specs=(
            P(None, "ctx", "head"),
            P(None, "ctx", "head"),
            P(None, "ctx", "head"),
            P("head", None, "ctx"),
            P("head", None, None),
            P("head", None, None),
            P("head", None, None),
            P("head", None),
            P("head", None),
        ),
        out_specs=P(None, "ctx", "head"),
        check_vma=False,
    )
```

```python
import functools
import jax
import jax.numpy as jnp
from jax import lax
from jax.experimental import pallas as pl
from jax.experimental.pallas import tpu as pltpu
from jax.sharding import PartitionSpec as P

WINDOW = 256
NS_ITERS = 5
MESH = pl.DeviceIdType.MESH
bf16 = jnp.bfloat16
f32 = jnp.float32

NN = (((1,), (0,)), ((), ()))
NT = (((1,), (1,)), ((), ()))
COPIES = 128


def split(x):
    high = x.astype(bf16)
    return high, (x - high.astype(f32)).astype(bf16)


def dot1(a, b, dims=NN):
    return lax.dot_general(a, b, dims, preferred_element_type=f32)


def dot3(a, b, dims=NN):
    axis = dims[0][1][0]
    left = jnp.concatenate([a[0], a[0], a[1]], axis=1)
    right = jnp.concatenate([b[0], b[1], b[0]], axis=axis)
    return dot1(left, right, dims)


def mirrored(whole, side):
    return whole + (side + side.T)


def unit_rows(x):
    return x / jnp.sqrt(jnp.sum(x * x, axis=-1, keepdims=True) + 1e-06)


def kernel(
    q_ref, k_ref, v_ref, rate_ref, gate_ref, up_ref, down_ref, gain_ref, proj_ref,
    out_ref,
    gate_now, up_now, down_now, part, yslot, xown, xslot, full, halo, attended, projg, gath, iterate,
    send_sem, recv_sem, local_sem,
):
    ctx = lax.axis_index("ctx")
    head = lax.axis_index("head")
    yi, xh = ctx // 2, ctx % 2
    xl, z, core = head // 8, (head // 2) % 4, head % 2
    first = ctx == 0

    barrier = pltpu.get_barrier_semaphore()
    for d in range(1, 8):
        pl.semaphore_signal(barrier, inc=1, device_id={"ctx": lax.rem(ctx + d, 8)}, device_id_type=MESH)
    for d in range(1, 16):
        pl.semaphore_signal(barrier, inc=1, device_id={"head": lax.rem(head + d, 16)}, device_id_type=MESH)

    started = []

    def send(src, dst, where):
        at = len(started)
        copy = pltpu.make_async_remote_copy(
            src_ref=src, dst_ref=dst, send_sem=send_sem.at[at], recv_sem=recv_sem.at[at],
            device_id=where, device_id_type=MESH,
        )
        copy.start()
        started.append(copy)
        return copy

    def rows64(index):
        return pl.ds(pl.multiple_of(index * 64, 64), 64)

    def halo_send(group):
        there = {"ctx": lax.rem(ctx + 1, 8)}
        return [
            send(ref.at[group, pl.ds(256, 256)], halo.at[group, at], there)
            for at, ref in enumerate((k_ref, v_ref))
        ]

    gate_now[...] = gate_ref[0]
    up_now[...] = up_ref[0]
    down_now[...] = down_ref[0].T

    def reduce_start(group, which, value):
        part[group, which] = value.astype(bf16)
        own = []
        for d in (2, 1, 3):
            there = lax.rem(yi + d, 4)
            own.append(
                send(
                    part.at[group, which, rows64(there)],
                    yslot.at[group, which, d - 1],
                    {"ctx": there * 2 + xh},
                )
            )
        return own

    def fast_grads(group, ready=None):
        key_unit = unit_rows(k_ref[group].astype(f32))
        key_two = split(key_unit)
        key_t = split(key_unit.T)
        gate_pre = dot3(key_two, split(gate_now[...]))
        up_pre = dot3(key_two, split(up_now[...]))
        if ready is not None:
            ready()
        rate_rows = jnp.broadcast_to(rate_ref[0, group : group + 1, :], (128, 512)).T[:, :1]
        target = rate_rows * v_ref[group].astype(f32)
        sigma = jax.nn.sigmoid(gate_pre)
        gate_act = gate_pre * sigma
        grad_down = dot3(split(target.T), split(gate_act * up_pre))
        sends = {2: reduce_start(group, 2, grad_down)}
        back = dot3(split(target), split(down_now[...]))
        sends[1] = reduce_start(group, 1, dot3(key_t, split(back * gate_act)))
        slope = sigma * (1.0 + gate_pre * (1.0 - sigma))
        sends[0] = reduce_start(group, 0, dot3(key_t, split(back * up_pre * slope)))
        return sends

    def reduce_second(group, which, sends):
        for copy in sends:
            copy.wait_recv()
        total = part[group, which, rows64(yi)].astype(f32)
        for slot in range(3):
            total = total + yslot[group, which, slot].astype(f32)
        xown[group, which] = total.astype(bf16)
        return send(xown.at[group, which], xslot.at[group, which], {"ctx": yi * 2 + (1 - xh)})

    def reduce_third(group, which, copy):
        copy.wait_recv()
        total = xown[group, which].astype(f32) + xslot[group, which].astype(f32)
        full[group, which, rows64(yi)] = total.astype(bf16)
        ref = full.at[group, which, rows64(yi)]
        return [send(ref, ref, {"ctx": lax.rem(yi + d, 4) * 2 + xh}) for d in (2, 1, 3)]

    def ortho_start(group, places):
        for at in places:
            grads = full[group, at].astype(f32)
            norm = jnp.sqrt(jnp.sum(grads * grads, keepdims=True)) + 1e-06
            iterate[at] = grads / norm

    def ortho_sweeps(places, count):
        def sweep(_, carry):
            x2 = {at: split(iterate[at]) for at in places}
            gram = {at: mirrored(dot1(x2[at][0], x2[at][0], NT), dot1(x2[at][0], x2[at][1], NT)) for at in places}
            g2 = {at: split(gram[at]) for at in places}
            poly = {
                at: -4.775 * gram[at] + 2.0315 * mirrored(dot1(g2[at][0], g2[at][0]), dot1(g2[at][0], g2[at][1]))
                for at in places
            }
            p2 = {at: split(poly[at]) for at in places}
            for at in places:
                iterate[at] = 3.4445 * iterate[at] + dot3(p2[at], x2[at])
            return carry

        lax.fori_loop(0, count, sweep, 0)

    def ortho_finish(places):
        for at in places:
            now = (gate_now, up_now, down_now)[at]
            now[...] = now[...] + 0.5 * iterate[at]

    def update(group, spread):
        for which in (2, 1, 0):
            for copy in spread[which]:
                copy.wait_recv()
        yield
        ortho_start(group, (2, 1, 0))
        ortho_sweeps((2, 1, 0), NS_ITERS)
        ortho_finish((2, 1, 0))
        yield

    def attend(group):
        if group == 0:
            prior = 0
        else:
            prior = jnp.where(first, 0, 1)
        query = unit_rows(q_ref[group].astype(f32)).astype(bf16)
        key = unit_rows(k_ref[group].astype(f32)).astype(bf16)
        halo_key = unit_rows(halo[prior, 0].astype(f32)).astype(bf16)
        query_pos = lax.broadcasted_iota(jnp.int32, (256, 512), 0)
        key_pos = lax.broadcasted_iota(jnp.int32, (256, 512), 1)
        distance = query_pos + WINDOW - key_pos
        band = (distance >= 0) & (distance < WINDOW)
        for block in range(2):
            if block == 0:
                keys = jnp.concatenate([halo_key, key[:256]], axis=0)
                vals = jnp.concatenate([halo[prior, 1], v_ref[group, 0:256]], axis=0)
            else:
                keys = key
                vals = v_ref[group]
            scores = dot1(query[block * 256 : block * 256 + 256], keys, NT)
            valid = band
            if block == 0 and group == 0:
                valid = band & (key_pos >= jnp.where(first, WINDOW, 0))
            weights = jnp.where(valid, jnp.exp(5.0 * (scores - 1.0)), 0.0)
            probs = (weights / jnp.sum(weights, axis=-1, keepdims=True)).astype(bf16)
            attended[group, block * 256 : block * 256 + 256] = dot1(probs, vals)

    def apply_fast(group, half):
        rows = pl.ds(half * 256, 256)
        query = split(unit_rows(q_ref[group, rows].astype(f32)))
        gate_pre = dot3(query, split(gate_now[...]))
        hidden = gate_pre * jax.nn.sigmoid(gate_pre) * dot3(query, split(up_now[...]))
        fast = dot3(split(hidden), split(down_now[...]), NT)
        normed = fast * lax.rsqrt(jnp.mean(fast * fast, axis=-1, keepdims=True) + 1e-05) * gain_ref[...]
        gath[group, head, rows] = (attended[group, rows] + normed).astype(bf16)

    def name(xl_at, z_at, core_at):
        return xl_at * 8 + lax.rem(z_at + 4, 4) * 2 + core_at

    sibling = {"head": name(xl, z, 1 - core)}
    above = {"head": name(xl, z + 1, core)}
    below = {"head": name(xl, z - 1, core)}
    across = {"head": name(1 - xl, z, core)}

    def block_send(group, owner, where, rows=None):
        ref = gath.at[group, owner] if rows is None else gath.at[group, owner, rows]
        return send(ref, ref, where)

    def half_rows(half):
        return pl.ds(half * 256, 256)

    def gather_z(group, half, c):
        c["zp", half] = block_send(group, head, above, half_rows(half))
        c["zm", half] = block_send(group, head, below, half_rows(half))

    def gather_x(group, half, c):
        c["x", half] = block_send(group, head, across, half_rows(half))

    def gather_sibling(group, c):
        c["sib"] = block_send(group, head, sibling)

    def relay_x(group, half, c):
        c["x", half].wait_recv()
        c["xp", half] = block_send(group, name(1 - xl, z, core), above, half_rows(half))
        c["xm", half] = block_send(group, name(1 - xl, z, core), below, half_rows(half))

    def relay_z(group, half, c):
        if half == 0:
            c["zp", 0].wait_recv()
            c["f", 0] = block_send(group, name(xl, z - 1, core), above, half_rows(0))
        else:
            c["zm", 1].wait_recv()
            c["f", 1] = block_send(group, name(xl, z + 1, core), below, half_rows(1))

    def relay_far(group, half, c):
        c["f", half].wait_recv()
        c["x2", half] = block_send(group, name(xl, z + 2, core), across, half_rows(half))

    def share_near(group, c):
        c["zp", 1].wait_recv()
        c["s1"] = block_send(group, name(xl, z - 1, core), sibling)
        c["zm", 0].wait_recv()
        c["s2"] = block_send(group, name(xl, z + 1, core), sibling)

    def share_across(group, c):
        c["s3"] = block_send(group, name(1 - xl, z, core), sibling)

    def share_far(group, c):
        c["s4"] = block_send(group, name(xl, z + 2, core), sibling)

    def share_sides(group, c):
        for half in range(2):
            c["xp", half].wait_recv()
        c["s5"] = block_send(group, name(1 - xl, z - 1, core), sibling)
        for half in range(2):
            c["xm", half].wait_recv()
        c["s6"] = block_send(group, name(1 - xl, z + 1, core), sibling)

    def share_last(group, c):
        for half in range(2):
            c["x2", half].wait_recv()
        c["s7"] = block_send(group, name(1 - xl, z + 2, core), sibling)

    own_order = (
        (xl, z), (xl, z - 1), (xl, z + 1), (1 - xl, z), (xl, z + 2), (1 - xl, z - 1), (1 - xl, z + 1), (1 - xl, z + 2)
    )
    shared = ("sib", "s1", "s2", "s3", "s4", "s5", "s6", "s7")

    def project(group, total, own, c):
        for at in own:
            owner = name(*own_order[at], core)
            term = dot1(gath[group, owner], projg[owner])
            total = term if total is None else total + term
        for at in own:
            c[shared[at]].wait_recv()
            owner = name(*own_order[at], 1 - core)
            total = total + dot1(gath[group, owner], projg[owner])
        return total

    mine = pltpu.make_async_copy(
        proj_ref.at[:, pl.ds(pl.multiple_of(head * 256, 256), 256)], projg.at[head], local_sem
    )
    exchange = []

    def exchange_with(there):
        exchange.append(
            send(
                proj_ref.at[:, pl.ds(pl.multiple_of(there * 256, 256), 256)],
                projg.at[head],
                {"head": there},
            )
        )

    def exchange_across(which):
        for d in which:
            exchange_with((1 - xl) * 8 + lax.rem(head + d, 8))

    def on_ready():
        pl.semaphore_wait(barrier, 22)
        mine.start()
        for d in range(1, 8):
            exchange_with(xl * 8 + lax.rem(head + d, 8))
        exchange_across(range(3))

    order = (2, 1, 0)
    sends = fast_grads(0, on_ready)
    cross = {which: reduce_second(0, which, sends[which]) for which in order}
    spread = {which: reduce_third(0, which, cross[which]) for which in order}
    steps = update(0, spread)
    next(steps)
    halos = [halo_send(0)]
    exchange_across(range(3, 8))
    next(steps)

    sends = fast_grads(1)
    near, last = {}, {}
    for copy in halos[0]:
        copy.wait_recv()
    attend(0)
    for half in range(2):
        apply_fast(0, half)
        gather_z(0, half, near)
    gather_sibling(0, near)
    cross = {which: reduce_second(1, which, sends[which]) for which in order}
    for half in range(2):
        gather_x(0, half, near)
    spread = {which: reduce_third(1, which, cross[which]) for which in order}
    for half in range(2):
        relay_z(0, half, near)
    steps = update(1, spread)
    next(steps)
    share_near(0, near)
    for half in range(2):
        relay_x(0, half, near)
        relay_far(0, half, near)
    share_across(0, near)
    share_far(0, near)
    halos.append(halo_send(1))
    next(steps)
    for copy in halos[1]:
        copy.wait_recv()
    attend(1)
    share_sides(0, near)
    share_last(0, near)
    for half in range(2):
        apply_fast(1, half)
        gather_x(1, half, last)
        gather_z(1, half, last)
    gather_sibling(1, last)
    mine.wait()
    for copy in exchange:
        copy.wait_recv()
    out_ref[0] = project(0, None, range(8), near).astype(bf16)
    for half in range(2):
        relay_x(1, half, last)
        relay_z(1, half, last)
    share_near(1, last)
    share_across(1, last)
    total = project(1, None, range(4), last)
    for half in range(2):
        relay_far(1, half, last)
    share_far(1, last)
    share_sides(1, last)
    total = project(1, total, range(4, 7), last)
    share_last(1, last)
    out_ref[1] = project(1, total, range(7, 8), last).astype(bf16)
    for copy in started:
        copy.wait_send()


def body(queries, keys, values, rates, w_gate, w_up, w_down, gains, out_proj):
    groups, rows, width = queries.shape
    hidden = w_gate.shape[2]
    vmem = pl.BlockSpec(memory_space=pltpu.VMEM)
    return pl.pallas_call(
        kernel,
        out_shape=jax.ShapeDtypeStruct((groups, rows, width), bf16),
        in_specs=[vmem] * 8 + [pl.BlockSpec(memory_space=pl.ANY)],
        out_specs=vmem,
        scratch_shapes=[
            pltpu.VMEM((width, hidden), f32),
            pltpu.VMEM((width, hidden), f32),
            pltpu.VMEM((width, hidden), f32),
            pltpu.VMEM((2, 3, width, hidden), bf16),
            pltpu.VMEM((2, 3, 3, 64, hidden), bf16),
            pltpu.VMEM((2, 3, 64, hidden), bf16),
            pltpu.VMEM((2, 3, 64, hidden), bf16),
            pltpu.VMEM((2, 3, width, hidden), bf16),
            pltpu.VMEM((2, 2, WINDOW, width), bf16),
            pltpu.VMEM((2, rows, width), f32),
            pltpu.VMEM((16, width, width), bf16),
            pltpu.VMEM((2, 16, rows, width), bf16),
            pltpu.VMEM((3, width, hidden), f32),
            pltpu.SemaphoreType.DMA((COPIES,)),
            pltpu.SemaphoreType.DMA((COPIES,)),
            pltpu.SemaphoreType.DMA,
        ],
        compiler_params=pltpu.CompilerParams(
            collective_id=0, has_side_effects=True, vmem_limit_bytes=62 * 1024 * 1024
        ),
    )(
        queries, keys, values, rates, w_gate, w_up, w_down, gains, out_proj
    )


def solution(mesh):
    return jax.shard_map(
        body,
        mesh=mesh,
        in_specs=(
            P(None, "ctx", "head"),
            P(None, "ctx", "head"),
            P(None, "ctx", "head"),
            P("head", None, "ctx"),
            P("head", None, None),
            P("head", None, None),
            P("head", None, None),
            P("head", None),
            P("head", None),
        ),
        out_specs=P(None, "ctx", "head"),
        check_vma=False,
    )
```

```python
import functools
import jax
import jax.numpy as jnp
from jax import lax
from jax.experimental import pallas as pl
from jax.experimental.pallas import tpu as pltpu
from jax.sharding import PartitionSpec as P

WINDOW = 256
NS_ITERS = 5
MESH = pl.DeviceIdType.MESH
bf16 = jnp.bfloat16
f32 = jnp.float32

NN = (((1,), (0,)), ((), ()))
NT = (((1,), (1,)), ((), ()))
COPIES = 128


def split(x):
    high = x.astype(bf16)
    return high, (x - high.astype(f32)).astype(bf16)


def dot1(a, b, dims=NN):
    return lax.dot_general(a, b, dims, preferred_element_type=f32)


def dot3(a, b, dims=NN):
    axis = dims[0][1][0]
    left = jnp.concatenate([a[0], a[0], a[1]], axis=1)
    right = jnp.concatenate([b[0], b[1], b[0]], axis=axis)
    return dot1(left, right, dims)


def mirrored(whole, side):
    return whole + (side + side.T)


def unit_rows(x):
    return x / jnp.sqrt(jnp.sum(x * x, axis=-1, keepdims=True) + 1e-06)


def kernel(
    q_ref, k_ref, v_ref, rate_ref, gate_ref, up_ref, down_ref, gain_ref, proj_ref,
    out_ref,
    gate_now, up_now, down_now, part, yslot, xown, xslot, full, halo, attended, projg, gath, iterate,
    send_sem, recv_sem, local_sem,
):
    ctx = lax.axis_index("ctx")
    head = lax.axis_index("head")
    yi, xh = ctx // 2, ctx % 2
    xl, z, core = head // 8, (head // 2) % 4, head % 2
    first = ctx == 0

    barrier = pltpu.get_barrier_semaphore()
    for d in range(1, 8):
        pl.semaphore_signal(barrier, inc=1, device_id={"ctx": lax.rem(ctx + d, 8)}, device_id_type=MESH)
    for d in range(1, 16):
        pl.semaphore_signal(barrier, inc=1, device_id={"head": lax.rem(head + d, 16)}, device_id_type=MESH)

    started = []

    def send(src, dst, where):
        at = len(started)
        copy = pltpu.make_async_remote_copy(
            src_ref=src, dst_ref=dst, send_sem=send_sem.at[at], recv_sem=recv_sem.at[at],
            device_id=where, device_id_type=MESH,
        )
        copy.start()
        started.append(copy)
        return copy

    def rows64(index):
        return pl.ds(pl.multiple_of(index * 64, 64), 64)

    def halo_send(group):
        there = {"ctx": lax.rem(ctx + 1, 8)}
        return [
            send(ref.at[group, pl.ds(256, 256)], halo.at[group, at], there)
            for at, ref in enumerate((k_ref, v_ref))
        ]

    gate_now[...] = gate_ref[0]
    up_now[...] = up_ref[0]
    down_now[...] = down_ref[0].T

    def reduce_start(group, which, value):
        part[group, which] = value.astype(bf16)
        own = []
        for d in (1, 3, 2):
            there = lax.rem(yi + d, 4)
            own.append(
                send(
                    part.at[group, which, rows64(there)],
                    yslot.at[group, which, d - 1],
                    {"ctx": there * 2 + xh},
                )
            )
        return own

    def fast_grads(group, ready=None):
        key_unit = unit_rows(k_ref[group].astype(f32))
        key_two = split(key_unit)
        key_t = split(key_unit.T)
        gate_pre = dot3(key_two, split(gate_now[...]))
        up_pre = dot3(key_two, split(up_now[...]))
        if ready is not None:
            ready()
        rate_rows = jnp.broadcast_to(rate_ref[0, group : group + 1, :], (128, 512)).T[:, :1]
        target = rate_rows * v_ref[group].astype(f32)
        sigma = jax.nn.sigmoid(gate_pre)
        gate_act = gate_pre * sigma
        grad_down = dot3(split(target.T), split(gate_act * up_pre))
        sends = {2: reduce_start(group, 2, grad_down)}
        back = dot3(split(target), split(down_now[...]))
        sends[1] = reduce_start(group, 1, dot3(key_t, split(back * gate_act)))
        slope = sigma * (1.0 + gate_pre * (1.0 - sigma))
        sends[0] = reduce_start(group, 0, dot3(key_t, split(back * up_pre * slope)))
        return sends

    def reduce_second(group, which, sends):
        for copy in sends:
            copy.wait_recv()
        total = part[group, which, rows64(yi)].astype(f32)
        for slot in range(3):
            total = total + yslot[group, which, slot].astype(f32)
        xown[group, which] = total.astype(bf16)
        return send(xown.at[group, which], xslot.at[group, which], {"ctx": yi * 2 + (1 - xh)})

    def reduce_third(group, which, copy):
        copy.wait_recv()
        total = xown[group, which].astype(f32) + xslot[group, which].astype(f32)
        full[group, which, rows64(yi)] = total.astype(bf16)
        ref = full.at[group, which, rows64(yi)]
        return [send(ref, ref, {"ctx": lax.rem(yi + d, 4) * 2 + xh}) for d in (1, 3, 2)]

    def ortho_start(group, places):
        for at in places:
            grads = full[group, at].astype(f32)
            norm = jnp.sqrt(jnp.sum(grads * grads, keepdims=True)) + 1e-06
            iterate[at] = grads / norm

    def ortho_sweeps(places, count):
        def sweep(_, carry):
            x2 = {at: split(iterate[at]) for at in places}
            gram = {at: mirrored(dot1(x2[at][0], x2[at][0], NT), dot1(x2[at][0], x2[at][1], NT)) for at in places}
            g2 = {at: split(gram[at]) for at in places}
            poly = {
                at: -4.775 * gram[at] + 2.0315 * mirrored(dot1(g2[at][0], g2[at][0]), dot1(g2[at][0], g2[at][1]))
                for at in places
            }
            p2 = {at: split(poly[at]) for at in places}
            for at in places:
                iterate[at] = 3.4445 * iterate[at] + dot3(p2[at], x2[at])
            return carry

        lax.fori_loop(0, count, sweep, 0)

    def ortho_finish(places):
        for at in places:
            now = (gate_now, up_now, down_now)[at]
            now[...] = now[...] + 0.5 * iterate[at]

    def update(group, spread):
        for which in (2, 1, 0):
            for copy in spread[which]:
                copy.wait_recv()
        yield
        ortho_start(group, (2, 1, 0))
        ortho_sweeps((2, 1, 0), NS_ITERS)
        ortho_finish((2, 1, 0))
        yield

    def attend(group):
        if group == 0:
            prior = 0
        else:
            prior = jnp.where(first, 0, 1)
        query = unit_rows(q_ref[group].astype(f32)).astype(bf16)
        key = unit_rows(k_ref[group].astype(f32)).astype(bf16)
        halo_key = unit_rows(halo[prior, 0].astype(f32)).astype(bf16)
        query_pos = lax.broadcasted_iota(jnp.int32, (256, 512), 0)
        key_pos = lax.broadcasted_iota(jnp.int32, (256, 512), 1)
        distance = query_pos + WINDOW - key_pos
        band = (distance >= 0) & (distance < WINDOW)
        for block in range(2):
            if block == 0:
                keys = jnp.concatenate([halo_key, key[:256]], axis=0)
                vals = jnp.concatenate([halo[prior, 1], v_ref[group, 0:256]], axis=0)
            else:
                keys = key
                vals = v_ref[group]
            scores = dot1(query[block * 256 : block * 256 + 256], keys, NT)
            valid = band
            if block == 0 and group == 0:
                valid = band & (key_pos >= jnp.where(first, WINDOW, 0))
            weights = jnp.where(valid, jnp.exp(5.0 * (scores - 1.0)), 0.0)
            probs = (weights / jnp.sum(weights, axis=-1, keepdims=True)).astype(bf16)
            attended[group, block * 256 : block * 256 + 256] = dot1(probs, vals)

    def apply_fast(group, half):
        rows = pl.ds(half * 256, 256)
        query = split(unit_rows(q_ref[group, rows].astype(f32)))
        gate_pre = dot3(query, split(gate_now[...]))
        hidden = gate_pre * jax.nn.sigmoid(gate_pre) * dot3(query, split(up_now[...]))
        fast = dot3(split(hidden), split(down_now[...]), NT)
        normed = fast * lax.rsqrt(jnp.mean(fast * fast, axis=-1, keepdims=True) + 1e-05) * gain_ref[...]
        gath[group, head, rows] = (attended[group, rows] + normed).astype(bf16)

    def name(xl_at, z_at, core_at):
        return xl_at * 8 + lax.rem(z_at + 4, 4) * 2 + core_at

    sibling = {"head": name(xl, z, 1 - core)}
    above = {"head": name(xl, z + 1, core)}
    below = {"head": name(xl, z - 1, core)}
    across = {"head": name(1 - xl, z, core)}

    def block_send(group, owner, where, rows=None):
        ref = gath.at[group, owner] if rows is None else gath.at[group, owner, rows]
        return send(ref, ref, where)

    def half_rows(half):
        return pl.ds(half * 256, 256)

    def gather_z(group, half, c):
        c["zp", half] = block_send(group, head, above, half_rows(half))
        c["zm", half] = block_send(group, head, below, half_rows(half))

    def gather_x(group, half, c):
        c["x", half] = block_send(group, head, across, half_rows(half))

    def gather_sibling(group, c):
        c["sib"] = block_send(group, head, sibling)

    def relay_x(group, half, c):
        c["x", half].wait_recv()
        c["xp", half] = block_send(group, name(1 - xl, z, core), above, half_rows(half))
        c["xm", half] = block_send(group, name(1 - xl, z, core), below, half_rows(half))

    def relay_z(group, half, c):
        if half == 0:
            c["zp", 0].wait_recv()
            c["f", 0] = block_send(group, name(xl, z - 1, core), above, half_rows(0))
        else:
            c["zm", 1].wait_recv()
            c["f", 1] = block_send(group, name(xl, z + 1, core), below, half_rows(1))

    def relay_far(group, half, c):
        c["f", half].wait_recv()
        c["x2", half] = block_send(group, name(xl, z + 2, core), across, half_rows(half))

    def share_near(group, c):
        c["zp", 1].wait_recv()
        c["s1"] = block_send(group, name(xl, z - 1, core), sibling)
        c["zm", 0].wait_recv()
        c["s2"] = block_send(group, name(xl, z + 1, core), sibling)

    def share_across(group, c):
        c["s3"] = block_send(group, name(1 - xl, z, core), sibling)

    def share_far(group, c):
        c["s4"] = block_send(group, name(xl, z + 2, core), sibling)

    def share_sides(group, c):
        for half in range(2):
            c["xp", half].wait_recv()
        c["s5"] = block_send(group, name(1 - xl, z - 1, core), sibling)
        for half in range(2):
            c["xm", half].wait_recv()
        c["s6"] = block_send(group, name(1 - xl, z + 1, core), sibling)

    def share_last(group, c):
        for half in range(2):
            c["x2", half].wait_recv()
        c["s7"] = block_send(group, name(1 - xl, z + 2, core), sibling)

    own_order = (
        (xl, z), (xl, z - 1), (xl, z + 1), (1 - xl, z), (xl, z + 2), (1 - xl, z - 1), (1 - xl, z + 1), (1 - xl, z + 2)
    )
    shared = ("sib", "s1", "s2", "s3", "s4", "s5", "s6", "s7")

    def project(group, total, own, c):
        for at in own:
            owner = name(*own_order[at], core)
            term = dot1(gath[group, owner], projg[owner])
            total = term if total is None else total + term
        for at in own:
            c[shared[at]].wait_recv()
            owner = name(*own_order[at], 1 - core)
            total = total + dot1(gath[group, owner], projg[owner])
        return total

    mine = pltpu.make_async_copy(
        proj_ref.at[:, pl.ds(pl.multiple_of(head * 256, 256), 256)], projg.at[head], local_sem
    )
    exchange = []

    def exchange_with(there):
        exchange.append(
            send(
                proj_ref.at[:, pl.ds(pl.multiple_of(there * 256, 256), 256)],
                projg.at[head],
                {"head": there},
            )
        )

    def exchange_across(which):
        for d in which:
            exchange_with((1 - xl) * 8 + lax.rem(head + d, 8))

    def on_ready():
        pl.semaphore_wait(barrier, 22)
        mine.start()
        for d in range(1, 8):
            exchange_with(xl * 8 + lax.rem(head + d, 8))
        exchange_across(range(3))

    order = (2, 1, 0)
    sends = fast_grads(0, on_ready)
    cross = {which: reduce_second(0, which, sends[which]) for which in order}
    spread = {which: reduce_third(0, which, cross[which]) for which in order}
    steps = update(0, spread)
    next(steps)
    halos = [halo_send(0)]
    exchange_across(range(3, 8))
    next(steps)

    sends = fast_grads(1)
    near, last = {}, {}
    for copy in halos[0]:
        copy.wait_recv()
    attend(0)
    for half in range(2):
        apply_fast(0, half)
        gather_z(0, half, near)
    gather_sibling(0, near)
    cross = {which: reduce_second(1, which, sends[which]) for which in order}
    for half in range(2):
        gather_x(0, half, near)
    spread = {which: reduce_third(1, which, cross[which]) for which in order}
    for half in range(2):
        relay_z(0, half, near)
    steps = update(1, spread)
    next(steps)
    share_near(0, near)
    for half in range(2):
        relay_x(0, half, near)
        relay_far(0, half, near)
    share_across(0, near)
    share_far(0, near)
    halos.append(halo_send(1))
    next(steps)
    for copy in halos[1]:
        copy.wait_recv()
    attend(1)
    share_sides(0, near)
    share_last(0, near)
    for half in range(2):
        apply_fast(1, half)
        gather_x(1, half, last)
        gather_z(1, half, last)
    gather_sibling(1, last)
    mine.wait()
    for copy in exchange:
        copy.wait_recv()
    out_ref[0] = project(0, None, range(8), near).astype(bf16)
    for half in range(2):
        relay_x(1, half, last)
        relay_z(1, half, last)
    share_near(1, last)
    share_across(1, last)
    total = project(1, None, range(4), last)
    for half in range(2):
        relay_far(1, half, last)
    share_far(1, last)
    share_sides(1, last)
    total = project(1, total, range(4, 7), last)
    share_last(1, last)
    out_ref[1] = project(1, total, range(7, 8), last).astype(bf16)
    for copy in started:
        copy.wait_send()


def body(queries, keys, values, rates, w_gate, w_up, w_down, gains, out_proj):
    groups, rows, width = queries.shape
    hidden = w_gate.shape[2]
    vmem = pl.BlockSpec(memory_space=pltpu.VMEM)
    return pl.pallas_call(
        kernel,
        out_shape=jax.ShapeDtypeStruct((groups, rows, width), bf16),
        in_specs=[vmem] * 8 + [pl.BlockSpec(memory_space=pl.ANY)],
        out_specs=vmem,
        scratch_shapes=[
            pltpu.VMEM((width, hidden), f32),
            pltpu.VMEM((width, hidden), f32),
            pltpu.VMEM((width, hidden), f32),
            pltpu.VMEM((2, 3, width, hidden), bf16),
            pltpu.VMEM((2, 3, 3, 64, hidden), bf16),
            pltpu.VMEM((2, 3, 64, hidden), bf16),
            pltpu.VMEM((2, 3, 64, hidden), bf16),
            pltpu.VMEM((2, 3, width, hidden), bf16),
            pltpu.VMEM((2, 2, WINDOW, width), bf16),
            pltpu.VMEM((2, rows, width), f32),
            pltpu.VMEM((16, width, width), bf16),
            pltpu.VMEM((2, 16, rows, width), bf16),
            pltpu.VMEM((3, width, hidden), f32),
            pltpu.SemaphoreType.DMA((COPIES,)),
            pltpu.SemaphoreType.DMA((COPIES,)),
            pltpu.SemaphoreType.DMA,
        ],
        compiler_params=pltpu.CompilerParams(
            collective_id=0, has_side_effects=True, vmem_limit_bytes=62 * 1024 * 1024
        ),
    )(
        queries, keys, values, rates, w_gate, w_up, w_down, gains, out_proj
    )


def solution(mesh):
    return jax.shard_map(
        body,
        mesh=mesh,
        in_specs=(
            P(None, "ctx", "head"),
            P(None, "ctx", "head"),
            P(None, "ctx", "head"),
            P("head", None, "ctx"),
            P("head", None, None),
            P("head", None, None),
            P("head", None, None),
            P("head", None),
            P("head", None),
        ),
        out_specs=P(None, "ctx", "head"),
        check_vma=False,
    )
```
